32 devices in a mesh: grid: 8 (over z, x), chan: 4 (over y, core).
Axes of the slice: x: 2, y: 2, z: 4, core: 2. Of those that a mesh axis runs over, the one named last changes fastest.
Arguments:
- input_field: bfloat16 [256, 1024, 1024], P('chan', 'grid'), may hold values from -6 to 6
- out_cotangent: bfloat16 [256, 1024, 1024], P('chan', 'grid'), may hold values from -6 to 6
- core_first: float32 [256, 16], replicated, may hold values from -1.5 to 1.5
- core_second: float32 [16, 256, 16], replicated, may hold values from -1.5 to 1.5
- core_third: float32 [16, 128, 16], replicated, may hold values from -1.5 to 1.5
- column_mode_core: float32 [2, 16, 128], replicated, may hold values from -2 to 2
Outputs:
- output_field: bfloat16 [256, 1024, 1024], P('chan', 'grid')
- input_grad: bfloat16 [256, 1024, 1024], P('chan', 'grid')
- grad_first: float32 [256, 16], replicated
- grad_second: float32 [16, 256, 16], replicated
- grad_third: float32 [16, 128, 16], replicated
- grad_fourth: float32 [2, 16, 128], replicated
The draws below stay inside these ranges and needn't reach their ends.
All inputs are finite; a program needn't handle non-finite values.
Results may differ from the reference program's by a relative error of at most 0.0079.
Values may be sent and summed in bfloat16 or wider, within the bound.
A program may use at most 128 MiB of HBM per device.

```python
import math
import jax
import jax.numpy as jnp
from jax import lax

CHANNELS = 256
GRID_SIDE = 1024
MODES_X = 128
MODES_Y = 128
RANK_ONE = 16
RANK_TWO = 16
RANK_THREE = 16


def block_scale(key, shape, split, smallest, top_value):
    factor_of, own = 1.0, jax.random.fold_in(key, 6)
    for position, shards_of in split:
        draws = jnp.exp(jax.random.uniform(jax.random.fold_in(own, position), (shards_of,), jnp.float32, smallest / len(split), top_value / len(split)))
        factor_of = factor_of * jnp.repeat(draws, shape[position] // shards_of).reshape([-1 if axis == position else 1 for axis in range(len(shape))])
    return factor_of


def centred(stream_key, shape, spread, most, split=(), kind=jnp.bfloat16):
    values = spread * jax.random.normal(stream_key, shape, jnp.float32)
    if split:
        values = values * block_scale(stream_key, shape, split, -0.22, 0.18)
    return jnp.clip(values, -most, most).astype(kind)


def setup_inputs(seed: int = 0) -> dict:
    keys = jax.random.split(jax.random.key(seed), 7)
    return {
        "input_field": centred(keys[0], (CHANNELS, GRID_SIDE, GRID_SIDE), 1.0, 6.0, ((0, 4), (1, 8))),
        "out_cotangent": centred(keys[1], (CHANNELS, GRID_SIDE, GRID_SIDE), 1.0, 6.0, ((0, 4), (1, 8))),
        "core_first": centred(keys[2], (CHANNELS, RANK_ONE), 0.25, 1.5, (), jnp.float32),
        "core_second": centred(keys[3], (RANK_ONE, CHANNELS, RANK_TWO), 0.25, 1.5, (), jnp.float32),
        "core_third": centred(keys[4], (RANK_TWO, MODES_X, RANK_THREE), 0.25, 1.5, (), jnp.float32),
        "column_mode_core": centred(keys[5], (2, RANK_THREE, MODES_Y), 0.35, 2.0, (), jnp.float32),
    }


full_turn = 2.0 * math.pi

def turn_tables(mode_index, row_index):
    freq = jnp.where(mode_index < MODES_X // 2, mode_index, GRID_SIDE - MODES_X + mode_index).astype(jnp.int32)
    phase = freq[:, None] * row_index[None, :] % GRID_SIDE
    angle = phase.astype(jnp.float32) * (full_turn / GRID_SIDE)
    cosine = jnp.cos(angle).astype(jnp.bfloat16)
    sine = jnp.sin(angle).astype(jnp.bfloat16)
    real_rows = jnp.stack([cosine, sine], axis=-1)
    imag_rows = jnp.stack([-sine, cosine], axis=-1)
    return jnp.stack([real_rows, imag_rows], axis=1)

def width_table():
    column = jnp.arange(GRID_SIDE, dtype=jnp.int32)
    wave = jnp.arange(MODES_Y, dtype=jnp.int32)
    phase = column[:, None] * wave[None, :] % GRID_SIDE
    angle = phase.astype(jnp.float32) * (full_turn / GRID_SIDE)
    cosine = jnp.cos(angle).astype(jnp.bfloat16)
    sine = jnp.sin(angle).astype(jnp.bfloat16)
    return jnp.stack([cosine, -sine], axis=1)

def mix_block(spec_block, third_core_block, core_first, core_second, column_mode_core):
    lead = jnp.einsum('ia,kiqy->kaqy', core_first, spec_block, precision=lax.Precision.HIGHEST)
    spectral_kernel = jnp.einsum('esz,pzm->sepm', third_core_block, column_mode_core, precision=lax.Precision.HIGHEST)
    inner = jnp.einsum('aob,kaqy->kobqy', core_second, lead, precision=lax.Precision.HIGHEST)
    kernel_re = spectral_kernel[:, None, :, 0, :]
    kernel_im = spectral_kernel[:, None, :, 1, :]
    inner_re = inner[:, :, :, 0, :]
    inner_im = inner[:, :, :, 1, :]
    out_re = lax.optimization_barrier(jnp.sum(inner_re * kernel_re - inner_im * kernel_im, axis=2))
    out_im = lax.optimization_barrier(jnp.sum(inner_re * kernel_im + inner_im * kernel_re, axis=2))
    return jnp.stack([out_re, out_im], axis=2)

def mix(spec_in, core_first, core_second, core_third, column_mode_core):
    blocks = spec_in.reshape(MODES_X // 8, 8, CHANNELS, 2, MODES_Y)
    third_blocks = core_third.reshape(RANK_TWO, MODES_X // 8, 8, RANK_THREE).transpose(1, 0, 2, 3)

    def one_block(pair):
        return mix_block(pair[0], pair[1], core_first, core_second, column_mode_core)
    result = lax.map(one_block, (blocks, third_blocks))
    return result.reshape(MODES_X, CHANNELS, 2, MODES_Y)

def rows_forward(field, table):
    blocks = field.reshape(16, CHANNELS // 16, GRID_SIDE, GRID_SIDE)

    def one_block(block):
        product = jnp.dot(block.reshape(-1, GRID_SIDE).astype(jnp.float32), table, precision=lax.Precision.HIGHEST)
        return product.astype(jnp.bfloat16).reshape(CHANNELS // 16, GRID_SIDE, 2, MODES_Y)
    return lax.map(one_block, blocks).reshape(CHANNELS, GRID_SIDE, 2, MODES_Y)

def rows_inverse(rows, table):
    blocks = rows.reshape(16, CHANNELS // 16 * GRID_SIDE, 2 * MODES_Y)

    def one_block(block):
        product = jnp.dot(block.astype(jnp.float32), table, precision=lax.Precision.HIGHEST)
        return (product * (1.0 / GRID_SIDE)).astype(jnp.bfloat16)
    return lax.map(one_block, blocks).reshape(CHANNELS, GRID_SIDE, GRID_SIDE)

def reference(input_field, out_cotangent, core_first, core_second, core_third, column_mode_core):
    base = width_table()
    forward_table = base.reshape(GRID_SIDE, 2 * MODES_Y).astype(jnp.float32)
    weight_c = jnp.where(jnp.arange(MODES_Y, dtype=jnp.int32) == 0, 1.0, 2.0).astype(jnp.float32)
    tables = turn_tables(jnp.arange(MODES_X, dtype=jnp.int32), jnp.arange(GRID_SIDE, dtype=jnp.int32)).astype(jnp.float32)

    def modes_of(rows):
        return jnp.einsum('kphq,chqy->kcpy', tables, rows.astype(jnp.float32), precision=lax.Precision.HIGHEST)
    spec_in = modes_of(rows_forward(input_field, forward_table)) * (1.0 / GRID_SIDE)
    spec_grad = modes_of(rows_forward(out_cotangent, forward_table)) * (weight_c / GRID_SIDE)
    spec_out, pullback = jax.vjp(mix, spec_in, core_first, core_second, core_third, column_mode_core)
    back_in, grad_one, grad_two, grad_three, grad_four = pullback(spec_grad)
    out_half = spec_out.astype(jnp.bfloat16)
    back_half = back_in.astype(jnp.bfloat16)
    inverse = tables.transpose(2, 3, 0, 1)

    def rows_of(modes):
        rows = jnp.einsum('hpkq,koqy->ohpy', inverse, modes.astype(jnp.float32), precision=lax.Precision.HIGHEST)
        return rows.astype(jnp.bfloat16)
    plain = base.transpose(1, 2, 0)
    weighted = plain * weight_c.astype(jnp.bfloat16)[None, :, None]
    output_field = rows_inverse(rows_of(out_half), weighted.reshape(2 * MODES_Y, GRID_SIDE).astype(jnp.float32))
    input_grad = rows_inverse(rows_of(back_half), plain.reshape(2 * MODES_Y, GRID_SIDE).astype(jnp.float32))
    scale = 1.0 / MODES_X
    return (output_field, input_grad, grad_one * scale, grad_two * scale, grad_three * scale, grad_four * scale)
```

```python
import math

import jax
import jax.numpy as jnp
import numpy as np
from jax import lax
from jax.experimental import pallas as pl
from jax.experimental.pallas import tpu as pltpu
from jax.sharding import PartitionSpec as P

F32 = jnp.float32
BF16 = jnp.bfloat16
HI = lax.Precision.HIGHEST
STEP = 16


def params(mib=48):
    return pltpu.CompilerParams(vmem_limit_bytes=mib * 2**20)


def dot(a, b, precision=None):
    return jnp.dot(a, b, preferred_element_type=F32, precision=precision)


def dot_nt(a, b, precision=None):
    return lax.dot_general(
        a, b, (((1,), (1,)), ((), ())), preferred_element_type=F32, precision=precision
    )


def dot_tn(a, b, precision=None):
    return lax.dot_general(
        a, b, (((0,), (0,)), ((), ())), preferred_element_type=F32, precision=precision
    )


def width_table(side, modes_y):
    phase = np.arange(side)[:, None] * np.arange(modes_y)[None, :] % side
    angle = phase.astype(np.float32) * np.float32(2.0 * math.pi / side)
    return np.concatenate([np.cos(angle), -np.sin(angle)], axis=1).astype(BF16)


def turn_table(side, modes_x):
    kx = np.arange(modes_x)
    freq = np.where(kx < modes_x // 2, kx, side - modes_x + kx)
    phase = freq[:, None] * np.arange(side)[None, :] % side
    angle = phase.astype(np.float32) * np.float32(2.0 * math.pi / side)
    return np.stack([np.cos(angle), np.sin(angle)]).astype(BF16)


def forward_turn(cs, block):
    x = dot(cs, block)
    n, m = x.shape[0] // 2, x.shape[1] // 2
    return x[:n, :m] + x[n:, m:], x[:n, m:] - x[n:, :m]


def inverse_turn(cs, block):
    x = dot(cs, block)
    n, m = x.shape[0] // 2, x.shape[1] // 2
    return x[:n, :m] - x[n:, m:], x[:n, m:] + x[n:, :m]


def spread(values, rows):
    n = values.shape[1]
    lane = lax.broadcasted_iota(jnp.int32, (n, n * STEP), 1)
    row = lax.broadcasted_iota(jnp.int32, (n, n * STEP), 0)
    wide = dot(values, (lane // STEP == row).astype(BF16))
    at = lax.broadcasted_iota(jnp.int32, (STEP, n * STEP), 1) % STEP
    unit = (at == lax.broadcasted_iota(jnp.int32, (STEP, n * STEP), 0)).astype(F32)
    return (wide[:, None, :] * unit[None]).reshape(rows * STEP, n * STEP).astype(BF16)


def lead_kernel(first_t, table, cs, field, modes, lead, kron, rows):
    step = pl.program_id(0)
    chan, _, side = field.shape
    rank = first_t.shape[0]
    wide = table.shape[1]

    @pl.when(step == 0)
    def _():
        kron[...] = spread(first_t[...], rank)

    product = dot(field[...].reshape(chan * STEP, side), table[...]).astype(BF16)
    modes[...] = product.reshape(chan, STEP, wide)
    mixed = dot(kron[...], product)
    rows[:, pl.ds(pl.multiple_of(step * STEP, STEP), STEP), :] = mixed.reshape(
        rank, STEP, wide
    ).astype(BF16)

    @pl.when(step == pl.num_programs(0) - 1)
    def _():
        half = wide // 2
        for a in range(rank):
            re, im = forward_turn(cs[...], rows[a])
            lead[a, :, :half] = re * (1.0 / side)
            lead[a, :, half:] = im * (1.0 / side)


def grad_kernel(table, cs, weight, field, spectrum, held):
    chan, rows, side = field.shape
    wide = table.shape[1]
    half = wide // 2
    product = dot(field[...].reshape(chan * rows, side), table[...]).astype(BF16)
    for c in range(chan):
        re, im = forward_turn(cs[...], product[c * rows : (c + 1) * rows])
        held[c, :, :half] = re * weight[:, :half]
        held[c, :, half:] = im * weight[:, half:]
    spectrum[...] = jnp.swapaxes(held[...], 0, 1).astype(BF16)


def back_kernel(second_ba, kernel, spectrum, out, held):
    rank_b = kernel.shape[1]
    rank_a = second_ba.shape[0] // rank_b
    half = kernel.shape[2] // 2

    def body(k, carry):
        g = dot(second_ba[...], spectrum[k])
        kr = kernel[k]
        re = jnp.zeros((rank_a, half), F32)
        im = jnp.zeros((rank_a, half), F32)
        for b in range(rank_b):
            gre = g[b * rank_a : (b + 1) * rank_a, :half]
            gim = g[b * rank_a : (b + 1) * rank_a, half:]
            kre, kim = kr[b : b + 1, :half], kr[b : b + 1, half:]
            re += gre * kre + gim * kim
            im += gim * kre - gre * kim
        held[k, :, :half] = re
        held[k, :, half:] = im
        return carry

    lax.fori_loop(0, STEP, body, 0, unroll=2)
    out[...] = jnp.swapaxes(held[...], 0, 1)


def mix_kernel(
    lead, kernel, spectrum, second_ab, second_t, third, column,
    out, part_second, part_third, part_fourth,
    lead_k, outer, out_k, kernel_grad,
):
    rank_a = lead.shape[0]
    rank_b = kernel.shape[1]
    half = kernel.shape[2] // 2
    lead_k[...] = jnp.swapaxes(lead[...], 0, 1)

    @pl.when(pl.program_id(0) == 0)
    def _():
        part_second[...] = jnp.zeros_like(part_second)
        part_fourth[...] = jnp.zeros_like(part_fourth)

    def body(k, carry):
        spec = spectrum[k]
        g = dot(second_ab[...], spec)
        kr, ld = kernel[k], lead_k[k]
        kre, kim = kr[:, :half], kr[:, half:]
        re = jnp.zeros((rank_b, half), F32)
        im = jnp.zeros((rank_b, half), F32)
        for a in range(rank_a):
            rows = slice(a * rank_b, (a + 1) * rank_b)
            lre, lim = ld[a : a + 1, :half], ld[a : a + 1, half:]
            outer[rows, :half] = (kre * lre - kim * lim).astype(BF16)
            outer[rows, half:] = (kre * lim + kim * lre).astype(BF16)
            gre, gim = g[rows, :half], g[rows, half:]
            re += gre * lre + gim * lim
            im += gim * lre - gre * lim
        at = pl.ds(pl.multiple_of(k * rank_b, rank_b), rank_b)
        kernel_grad[at, :half] = re
        kernel_grad[at, half:] = im
        out_k[k] = dot(second_t[...], outer[...])
        part_second[...] += dot_nt(spec, outer[...])
        return carry

    lax.fori_loop(0, STEP, body, 0, unroll=2)
    out[...] = jnp.swapaxes(out_k[...], 0, 1).astype(BF16)
    part_third[0] = dot_nt(column[...], kernel_grad[...], HI)
    part_fourth[...] += dot_tn(third[...], kernel_grad[...], HI)


def field_kernel(cs, table, spectrum, out, rows):
    chan = spectrum.shape[0]
    n = out.shape[1]
    half = table.shape[0] // 2
    lane = lax.broadcasted_iota(jnp.int32, (n, half), 1)
    scale = jnp.where(lane == 0, 1.0, 2.0) * (1.0 / table.shape[1])
    for c in range(chan):
        re, im = inverse_turn(cs[...], spectrum[c])
        rows[c * n : (c + 1) * n, :half] = (re * scale).astype(BF16)
        rows[c * n : (c + 1) * n, half:] = (im * scale).astype(BF16)
        out[c] = dot(rows[c * n : (c + 1) * n, :], table[...]).astype(BF16)


def first_kernel(cs, lead_grad, modes, rows, part_first, total):
    step = pl.program_id(0)
    rank, n, wide = rows.shape
    chan = modes.shape[0]
    half = wide // 2

    @pl.when(step == 0)
    def _():
        total[...] = jnp.zeros_like(total)
        for a in range(rank):
            re, im = inverse_turn(cs[...], lead_grad[a].astype(BF16))
            rows[a, :, :half] = re.astype(BF16)
            rows[a, :, half:] = im.astype(BF16)

    at = pl.ds(pl.multiple_of(step * STEP, STEP), STEP)
    block = rows[:, at, :].reshape(rank * STEP, wide)
    total[...] += dot_nt(modes[...].reshape(chan * STEP, wide), block)

    @pl.when(step == pl.num_programs(0) - 1)
    def _():
        shape = (STEP, rank * STEP)
        unit = lax.broadcasted_iota(jnp.int32, shape, 1) % STEP == lax.broadcasted_iota(
            jnp.int32, shape, 0
        )
        kept = total[...].reshape(chan, STEP, rank * STEP) * unit.astype(F32)[None]
        lane = lax.broadcasted_iota(jnp.int32, (rank, rank * STEP), 1)
        row = lax.broadcasted_iota(jnp.int32, (rank, rank * STEP), 0)
        pick = (lane // STEP == row).astype(F32)
        part_first[...] = dot_nt(pick, jnp.sum(kept, axis=1), HI)


def input_kernel(first, table, rows, out, kron):
    rank, _, wide = rows.shape
    chan, _, side = out.shape

    @pl.when(pl.program_id(0) == 0)
    def _():
        kron[...] = spread(first[...], chan)

    block = dot(kron[...], rows[...].reshape(rank * STEP, wide)) * (1.0 / side)
    out[...] = dot(block.astype(BF16), table[...]).astype(BF16).reshape(out.shape)


def whole(shape):
    return pl.BlockSpec(shape, lambda i: (0,) * len(shape))


def sum_all(x):
    return lax.psum(x, ("grid", "chan"))


def local(input_field, out_cotangent, core_first, core_second, core_third, column_mode_core):
    grid_count = lax.axis_size("grid")
    grid_index = lax.axis_index("grid")
    chan_index = lax.axis_index("chan")
    chan, rows, side = input_field.shape
    channels, rank_a = core_first.shape
    rank_b, modes_x, rank_d = core_third.shape
    modes_y = column_mode_core.shape[2]
    wide = 2 * modes_y

    table_np = width_table(side, modes_y)
    table = jnp.asarray(table_np)
    table_t = jnp.asarray(np.ascontiguousarray(table_np.T))
    turns = turn_table(side, modes_x).reshape(2, modes_x, grid_count, rows)
    forward = np.ascontiguousarray(turns.transpose(2, 0, 1, 3)).reshape(
        grid_count, 2 * modes_x, rows
    )
    backward = np.ascontiguousarray(turns.transpose(2, 0, 3, 1)).reshape(
        grid_count, 2 * rows, modes_x
    )
    cs = lax.dynamic_index_in_dim(jnp.asarray(forward), grid_index, 0, keepdims=False)
    cs_t = lax.dynamic_index_in_dim(jnp.asarray(backward), grid_index, 0, keepdims=False)
    weight_c = np.where(np.arange(wide) % modes_y == 0, 1.0, 2.0).astype(np.float32)
    weight = jnp.asarray((weight_c / side)[None, :])

    first_local = lax.dynamic_slice_in_dim(core_first, chan_index * chan, chan, 0)
    second_local = lax.dynamic_slice_in_dim(core_second, chan_index * chan, chan, 1)
    first_bf = first_local.astype(BF16)
    second_bf = second_local.astype(BF16)
    pairs = rank_a * rank_b
    second_ab = second_bf.transpose(0, 2, 1).reshape(pairs, chan)
    second_ba = second_bf.transpose(2, 0, 1).reshape(pairs, chan)
    second_t = second_bf.transpose(1, 0, 2).reshape(chan, pairs)
    third_rows = core_third.transpose(1, 0, 2).reshape(modes_x * rank_b, rank_d)
    column = column_mode_core.transpose(1, 0, 2).reshape(rank_d, wide)
    kernel = dot(third_rows, column, HI).reshape(modes_x, rank_b, wide)

    row_steps = rows // STEP
    mode_steps = modes_x // STEP
    chan_step = min(chan, STEP)
    out_step = min(chan, 8)

    row_modes, lead = pl.pallas_call(
        lead_kernel,
        grid=(row_steps,),
        in_specs=[
            whole((rank_a, chan)),
            whole((side, wide)),
            whole((2 * modes_x, rows)),
            pl.BlockSpec((chan, STEP, side), lambda i: (0, i, 0)),
        ],
        out_specs=[
            pl.BlockSpec((chan, STEP, wide), lambda i: (0, i, 0)),
            whole((rank_a, modes_x, wide)),
        ],
        out_shape=[
            jax.ShapeDtypeStruct((chan, rows, wide), BF16),
            jax.ShapeDtypeStruct((rank_a, modes_x, wide), F32),
        ],
        scratch_shapes=[
            pltpu.VMEM((rank_a * STEP, chan * STEP), BF16),
            pltpu.VMEM((rank_a, rows, wide), BF16),
        ],
        compiler_params=params(),
        name="lead",
    )(first_bf.T, table, cs, input_field)
    lead = sum_all(lead)

    spec_grad = pl.pallas_call(
        grad_kernel,
        grid=(chan // chan_step,),
        in_specs=[
            whole((side, wide)),
            whole((2 * modes_x, rows)),
            whole((1, wide)),
            pl.BlockSpec((chan_step, rows, side), lambda i: (i, 0, 0)),
        ],
        out_specs=pl.BlockSpec((modes_x, chan_step, wide), lambda i: (0, i, 0)),
        out_shape=jax.ShapeDtypeStruct((modes_x, chan, wide), BF16),
        scratch_shapes=[pltpu.VMEM((chan_step, modes_x, wide), F32)],
        compiler_params=params(),
        name="spec_grad",
    )(table, cs, weight, out_cotangent)

    lead_grad = pl.pallas_call(
        back_kernel,
        grid=(mode_steps,),
        in_specs=[
            whole((pairs, chan)),
            pl.BlockSpec((STEP, rank_b, wide), lambda i: (i, 0, 0)),
            pl.BlockSpec((STEP, chan, wide), lambda i: (i, 0, 0)),
        ],
        out_specs=pl.BlockSpec((rank_a, STEP, wide), lambda i: (0, i, 0)),
        out_shape=jax.ShapeDtypeStruct((rank_a, modes_x, wide), F32),
        scratch_shapes=[pltpu.VMEM((STEP, rank_a, wide), F32)],
        compiler_params=params(),
        name="lead_grad",
    )(second_ba, kernel, spec_grad)
    lead_grad = sum_all(lead_grad)

    spec_out, part_second, part_third, part_fourth = pl.pallas_call(
        mix_kernel,
        grid=(mode_steps,),
        in_specs=[
            pl.BlockSpec((rank_a, STEP, wide), lambda i: (0, i, 0)),
            pl.BlockSpec((STEP, rank_b, wide), lambda i: (i, 0, 0)),
            pl.BlockSpec((STEP, chan, wide), lambda i: (i, 0, 0)),
            whole((pairs, chan)),
            whole((chan, pairs)),
            pl.BlockSpec((STEP * rank_b, rank_d), lambda i: (i, 0)),
            whole((rank_d, wide)),
        ],
        out_specs=[
            pl.BlockSpec((chan, STEP, wide), lambda i: (0, i, 0)),
            whole((chan, pairs)),
            pl.BlockSpec((1, rank_d, STEP * rank_b), lambda i: (i, 0, 0)),
            whole((rank_d, wide)),
        ],
        out_shape=[
            jax.ShapeDtypeStruct((chan, modes_x, wide), BF16),
            jax.ShapeDtypeStruct((chan, pairs), F32),
            jax.ShapeDtypeStruct((mode_steps, rank_d, STEP * rank_b), F32),
            jax.ShapeDtypeStruct((rank_d, wide), F32),
        ],
        scratch_shapes=[
            pltpu.VMEM((STEP, rank_a, wide), F32),
            pltpu.VMEM((pairs, wide), BF16),
            pltpu.VMEM((STEP, chan, wide), F32),
            pltpu.VMEM((STEP * rank_b, wide), F32),
        ],
        compiler_params=params(),
        name="mix",
    )(lead, kernel, spec_grad, second_ab, second_t, third_rows, column)

    back_rows, part_first = pl.pallas_call(
        first_kernel,
        grid=(row_steps,),
        in_specs=[
            whole((2 * rows, modes_x)),
            whole((rank_a, modes_x, wide)),
            pl.BlockSpec((chan, STEP, wide), lambda i: (0, i, 0)),
        ],
        out_specs=[whole((rank_a, rows, wide)), whole((rank_a, chan))],
        out_shape=[
            jax.ShapeDtypeStruct((rank_a, rows, wide), BF16),
            jax.ShapeDtypeStruct((rank_a, chan), F32),
        ],
        scratch_shapes=[pltpu.VMEM((chan * STEP, rank_a * STEP), F32)],
        compiler_params=params(),
        name="first",
    )(cs_t, lead_grad, row_modes)

    first_wide = lax.dynamic_update_slice(
        jnp.zeros((rank_a, channels), F32), part_first * (1.0 / side), (0, chan_index * chan)
    )
    second_wide = lax.dynamic_update_slice(
        jnp.zeros((channels, pairs), F32), part_second, (chan_index * chan, 0)
    )
    sizes = [first_wide.size, second_wide.size, part_third.size, part_fourth.size]
    packed = jnp.concatenate(
        [v.reshape(-1, wide) for v in (first_wide, second_wide, part_third, part_fourth)]
    )
    packed = sum_all(packed) * (1.0 / modes_x)
    cuts = np.cumsum([0] + [s // wide for s in sizes])
    one, two, three, four = (packed[cuts[n] : cuts[n + 1]] for n in range(4))
    grad_first = one.reshape(rank_a, channels).T
    grad_second = two.reshape(channels, rank_a, rank_b).transpose(1, 0, 2)
    grad_third = (
        three.reshape(mode_steps, rank_d, STEP, rank_b)
        .transpose(3, 0, 2, 1)
        .reshape(rank_b, modes_x, rank_d)
    )
    grad_fourth = four.reshape(rank_d, 2, modes_y).transpose(1, 0, 2)

    output_field = pl.pallas_call(
        field_kernel,
        grid=(chan // out_step,),
        in_specs=[
            whole((2 * rows, modes_x)),
            whole((wide, side)),
            pl.BlockSpec((out_step, modes_x, wide), lambda i: (i, 0, 0)),
        ],
        out_specs=pl.BlockSpec((out_step, rows, side), lambda i: (i, 0, 0)),
        out_shape=jax.ShapeDtypeStruct((chan, rows, side), BF16),
        scratch_shapes=[pltpu.VMEM((out_step * rows, wide), BF16)],
        compiler_params=params(),
        name="output",
    )(cs_t, table_t, spec_out)

    input_grad = pl.pallas_call(
        input_kernel,
        grid=(row_steps,),
        in_specs=[
            whole((chan, rank_a)),
            whole((wide, side)),
            pl.BlockSpec((rank_a, STEP, wide), lambda i: (0, i, 0)),
        ],
        out_specs=pl.BlockSpec((chan, STEP, side), lambda i: (0, i, 0)),
        out_shape=jax.ShapeDtypeStruct((chan, rows, side), BF16),
        scratch_shapes=[pltpu.VMEM((chan * STEP, rank_a * STEP), BF16)],
        compiler_params=params(),
        name="input_grad",
    )(first_bf, table_t, back_rows)

    return output_field, input_grad, grad_first, grad_second, grad_third, grad_fourth


def solution(mesh):
    placed = (P("chan", "grid", None), P("chan", "grid", None), P(), P(), P(), P())
    return jax.shard_map(
        local,
        mesh=mesh,
        in_specs=placed,
        out_specs=(P("chan", "grid", None), P("chan", "grid", None), P(), P(), P(), P()),
        check_vma=False,
    )
```

```python
import math

import jax
import jax.numpy as jnp
import numpy as np
from jax import lax
from jax.experimental import pallas as pl
from jax.experimental.pallas import tpu as pltpu
from jax.sharding import PartitionSpec as P

F32 = jnp.float32
BF16 = jnp.bfloat16
HI = lax.Precision.HIGHEST
STEP = 16


def params(mib=48):
    return pltpu.CompilerParams(vmem_limit_bytes=mib * 2**20)


def dot(a, b, precision=None):
    return jnp.dot(a, b, preferred_element_type=F32, precision=precision)


def dot_nt(a, b, precision=None):
    return lax.dot_general(
        a, b, (((1,), (1,)), ((), ())), preferred_element_type=F32, precision=precision
    )


def dot_tn(a, b, precision=None):
    return lax.dot_general(
        a, b, (((0,), (0,)), ((), ())), preferred_element_type=F32, precision=precision
    )


def width_table(side, modes_y):
    phase = np.arange(side)[:, None] * np.arange(modes_y)[None, :] % side
    angle = phase.astype(np.float32) * np.float32(2.0 * math.pi / side)
    return np.concatenate([np.cos(angle), -np.sin(angle)], axis=1).astype(BF16)


def turn_table(side, modes_x):
    kx = np.arange(modes_x)
    freq = np.where(kx < modes_x // 2, kx, side - modes_x + kx)
    phase = freq[:, None] * np.arange(side)[None, :] % side
    angle = phase.astype(np.float32) * np.float32(2.0 * math.pi / side)
    return np.stack([np.cos(angle), np.sin(angle)]).astype(BF16)


def forward_turn(cs, block):
    x = dot(cs, block)
    n, m = x.shape[0] // 2, x.shape[1] // 2
    return x[:n, :m] + x[n:, m:], x[:n, m:] - x[n:, :m]


def inverse_turn(cs, block):
    x = dot(cs, block)
    n, m = x.shape[0] // 2, x.shape[1] // 2
    return x[:n, :m] - x[n:, m:], x[:n, m:] + x[n:, :m]


def spread(values, rows):
    n = values.shape[1]
    lane = lax.broadcasted_iota(jnp.int32, (n, n * STEP), 1)
    row = lax.broadcasted_iota(jnp.int32, (n, n * STEP), 0)
    wide = dot(values, (lane // STEP == row).astype(BF16))
    at = lax.broadcasted_iota(jnp.int32, (STEP, n * STEP), 1) % STEP
    unit = (at == lax.broadcasted_iota(jnp.int32, (STEP, n * STEP), 0)).astype(F32)
    return (wide[:, None, :] * unit[None]).reshape(rows * STEP, n * STEP).astype(BF16)


def lead_kernel(first_t, table, cs, field, modes, lead, kron, rows):
    step = pl.program_id(0)
    chan, _, side = field.shape
    rank = first_t.shape[0]
    wide = table.shape[1]

    @pl.when(step == 0)
    def _():
        kron[...] = spread(first_t[...], rank)

    product = dot(field[...].reshape(chan * STEP, side), table[...]).astype(BF16)
    modes[...] = product.reshape(chan, STEP, wide)
    mixed = dot(kron[...], product)
    rows[:, pl.ds(pl.multiple_of(step * STEP, STEP), STEP), :] = mixed.reshape(
        rank, STEP, wide
    ).astype(BF16)

    @pl.when(step == pl.num_programs(0) - 1)
    def _():
        half = wide // 2
        for a in range(rank):
            re, im = forward_turn(cs[...], rows[a])
            lead[a, :, :half] = re * (1.0 / side)
            lead[a, :, half:] = im * (1.0 / side)


def grad_kernel(table, cs, weight, field, spectrum, held):
    chan, rows, side = field.shape
    wide = table.shape[1]
    half = wide // 2
    product = dot(field[...].reshape(chan * rows, side), table[...]).astype(BF16)
    for c in range(chan):
        re, im = forward_turn(cs[...], product[c * rows : (c + 1) * rows])
        held[c, :, :half] = re * weight[:, :half]
        held[c, :, half:] = im * weight[:, half:]
    spectrum[...] = jnp.swapaxes(held[...], 0, 1).astype(BF16)


def back_kernel(second_ba, kernel, spectrum, out, held):
    rank_b = kernel.shape[1]
    rank_a = second_ba.shape[0] // rank_b
    half = kernel.shape[2] // 2

    def body(k, carry):
        g = dot(second_ba[...], spectrum[k])
        kr = kernel[k]
        re = jnp.zeros((rank_a, half), F32)
        im = jnp.zeros((rank_a, half), F32)
        for b in range(rank_b):
            gre = g[b * rank_a : (b + 1) * rank_a, :half]
            gim = g[b * rank_a : (b + 1) * rank_a, half:]
            kre, kim = kr[b : b + 1, :half], kr[b : b + 1, half:]
            re += gre * kre + gim * kim
            im += gim * kre - gre * kim
        held[k, :, :half] = re
        held[k, :, half:] = im
        return carry

    lax.fori_loop(0, STEP, body, 0, unroll=2)
    out[...] = jnp.swapaxes(held[...], 0, 1)


def mix_kernel(
    lead, kernel, spectrum, second_ab, second_t, third, column,
    out, part_second, part_third, part_fourth,
    lead_k, outer, out_k, kernel_grad,
):
    rank_a = lead.shape[0]
    rank_b = kernel.shape[1]
    half = kernel.shape[2] // 2
    lead_k[...] = jnp.swapaxes(lead[...], 0, 1)

    @pl.when(pl.program_id(0) == 0)
    def _():
        part_second[...] = jnp.zeros_like(part_second)
        part_fourth[...] = jnp.zeros_like(part_fourth)

    def body(k, carry):
        spec = spectrum[k]
        g = dot(second_ab[...], spec)
        kr, ld = kernel[k], lead_k[k]
        kre, kim = kr[:, :half], kr[:, half:]
        re = jnp.zeros((rank_b, half), F32)
        im = jnp.zeros((rank_b, half), F32)
        for a in range(rank_a):
            rows = slice(a * rank_b, (a + 1) * rank_b)
            lre, lim = ld[a : a + 1, :half], ld[a : a + 1, half:]
            outer[rows, :half] = (kre * lre - kim * lim).astype(BF16)
            outer[rows, half:] = (kre * lim + kim * lre).astype(BF16)
            gre, gim = g[rows, :half], g[rows, half:]
            re += gre * lre + gim * lim
            im += gim * lre - gre * lim
        at = pl.ds(pl.multiple_of(k * rank_b, rank_b), rank_b)
        kernel_grad[at, :half] = re
        kernel_grad[at, half:] = im
        out_k[k] = dot(second_t[...], outer[...])
        part_second[...] += dot_nt(spec, outer[...])
        return carry

    lax.fori_loop(0, STEP, body, 0, unroll=2)
    out[...] = jnp.swapaxes(out_k[...], 0, 1).astype(BF16)
    part_third[0] = dot_nt(column[...], kernel_grad[...], HI)
    part_fourth[...] += dot_tn(third[...], kernel_grad[...], HI)


def field_kernel(cs, table, spectrum, out, rows):
    chan = spectrum.shape[0]
    n = out.shape[1]
    half = table.shape[0] // 2
    lane = lax.broadcasted_iota(jnp.int32, (n, half), 1)
    scale = jnp.where(lane == 0, 1.0, 2.0) * (1.0 / table.shape[1])
    for c in range(chan):
        re, im = inverse_turn(cs[...], spectrum[c])
        rows[c * n : (c + 1) * n, :half] = (re * scale).astype(BF16)
        rows[c * n : (c + 1) * n, half:] = (im * scale).astype(BF16)
        out[c] = dot(rows[c * n : (c + 1) * n, :], table[...]).astype(BF16)


def first_kernel(cs, lead_grad, modes, rows, part_first, total):
    step = pl.program_id(0)
    rank, n, wide = rows.shape
    chan = modes.shape[0]
    half = wide // 2

    @pl.when(step == 0)
    def _():
        total[...] = jnp.zeros_like(total)
        for a in range(rank):
            re, im = inverse_turn(cs[...], lead_grad[a].astype(BF16))
            rows[a, :, :half] = re.astype(BF16)
            rows[a, :, half:] = im.astype(BF16)

    at = pl.ds(pl.multiple_of(step * STEP, STEP), STEP)
    block = rows[:, at, :].reshape(rank * STEP, wide)
    total[...] += dot_nt(modes[...].reshape(chan * STEP, wide), block)

    @pl.when(step == pl.num_programs(0) - 1)
    def _():
        shape = (STEP, rank * STEP)
        unit = lax.broadcasted_iota(jnp.int32, shape, 1) % STEP == lax.broadcasted_iota(
            jnp.int32, shape, 0
        )
        kept = total[...].reshape(chan, STEP, rank * STEP) * unit.astype(F32)[None]
        lane = lax.broadcasted_iota(jnp.int32, (rank, rank * STEP), 1)
        row = lax.broadcasted_iota(jnp.int32, (rank, rank * STEP), 0)
        pick = (lane // STEP == row).astype(F32)
        part_first[...] = dot_nt(pick, jnp.sum(kept, axis=1), HI)


def input_kernel(first, table, rows, out, kron):
    rank, _, wide = rows.shape
    chan, _, side = out.shape

    @pl.when(pl.program_id(0) == 0)
    def _():
        kron[...] = spread(first[...], chan)

    block = dot(kron[...], rows[...].reshape(rank * STEP, wide)) * (1.0 / side)
    out[...] = dot(block.astype(BF16), table[...]).astype(BF16).reshape(out.shape)


def whole(shape):
    return pl.BlockSpec(shape, lambda i: (0,) * len(shape))


def halvings(order, units):
    start, size, plan = 0, units, []
    for axis, bit in order:
        size //= 2
        side = lax.axis_index(axis) // bit % 2
        plan.append((axis, bit, side, start + side * size, start + (1 - side) * size, size))
        start = start + side * size
    return plan


def partner(axis, bit, side):
    return {axis: lax.axis_index(axis) + bit * (1 - 2 * side)}


def reduce_kernel(orders, *refs):
    count = len(orders)
    inputs, outputs = refs[:count], refs[count : 2 * count]
    totals, landed = refs[2 * count : 3 * count], refs[3 * count : 4 * count]
    send_sem, recv_sem = refs[4 * count :]
    plans = [halvings(order, ref.shape[0]) for order, ref in zip(orders, inputs)]
    steps = len(orders[0])
    barrier = pltpu.get_barrier_semaphore()
    for axis, bit, side, *_ in plans[0]:
        pl.semaphore_signal(
            barrier, inc=1, device_id=partner(axis, bit, side),
            device_id_type=pl.DeviceIdType.MESH,
        )
    pl.semaphore_wait(barrier, steps)

    for step in range(steps):
        copies = []
        for c in range(count):
            axis, bit, side, _, other, size = plans[c][step]
            source = inputs[c] if step == 0 else totals[c]
            first = inputs[c].shape[0] - 2 * size
            copy = pltpu.make_async_remote_copy(
                src_ref=source.at[pl.ds(other, size)],
                dst_ref=landed[c].at[pl.ds(first, size)],
                send_sem=send_sem.at[0, c, step],
                recv_sem=recv_sem.at[0, c, step],
                device_id=partner(axis, bit, side),
                device_id_type=pl.DeviceIdType.MESH,
            )
            copy.start()
            copies.append(copy)
        for c in range(count):
            _, _, _, own, _, size = plans[c][step]
            source = inputs[c] if step == 0 else totals[c]
            target = outputs[c] if step == steps - 1 else totals[c]
            first = inputs[c].shape[0] - 2 * size
            copies[c].wait()
            target[pl.ds(own, size)] = source[pl.ds(own, size)] + landed[c][pl.ds(first, size)]

    for step in reversed(range(steps)):
        copies = []
        for c in range(count):
            axis, bit, side, own, _, size = plans[c][step]
            copy = pltpu.make_async_remote_copy(
                src_ref=outputs[c].at[pl.ds(own, size)],
                dst_ref=outputs[c].at[pl.ds(own, size)],
                send_sem=send_sem.at[1, c, step],
                recv_sem=recv_sem.at[1, c, step],
                device_id=partner(axis, bit, side),
                device_id_type=pl.DeviceIdType.MESH,
            )
            copy.start()
            copies.append(copy)
        for copy in copies:
            copy.wait()


def bits(axis):
    return [(axis, 1 << n) for n in range((lax.axis_size(axis) - 1).bit_length())]


def sum_all(arrays, collective_id):
    chan, grid = bits("chan"), bits("grid")
    orders = [chan + grid, chan[:1] + grid + chan[1:]][: len(arrays)]
    wide = arrays[0].shape[-1]
    flat = [a.reshape(-1, 8, wide) for a in arrays]
    vmem = pl.BlockSpec(memory_space=pltpu.VMEM)
    results = pl.pallas_call(
        lambda *refs: reduce_kernel(orders, *refs),
        in_specs=[vmem] * len(flat),
        out_specs=[vmem] * len(flat),
        out_shape=[jax.ShapeDtypeStruct(a.shape, F32) for a in flat],
        scratch_shapes=[pltpu.VMEM(a.shape, F32) for a in flat]
        + [pltpu.VMEM(a.shape, F32) for a in flat]
        + [pltpu.SemaphoreType.DMA((2, len(flat), len(orders[0])))] * 2,
        compiler_params=pltpu.CompilerParams(
            collective_id=collective_id, has_side_effects=True, vmem_limit_bytes=48 * 2**20
        ),
        name="sum_all",
    )(*flat)
    return [r.reshape(a.shape) for r, a in zip(results, arrays)]


def local(input_field, out_cotangent, core_first, core_second, core_third, column_mode_core):
    grid_count = lax.axis_size("grid")
    grid_index = lax.axis_index("grid")
    chan_index = lax.axis_index("chan")
    chan, rows, side = input_field.shape
    channels, rank_a = core_first.shape
    rank_b, modes_x, rank_d = core_third.shape
    modes_y = column_mode_core.shape[2]
    wide = 2 * modes_y

    table_np = width_table(side, modes_y)
    table = jnp.asarray(table_np)
    table_t = jnp.asarray(np.ascontiguousarray(table_np.T))
    turns = turn_table(side, modes_x).reshape(2, modes_x, grid_count, rows)
    forward = np.ascontiguousarray(turns.transpose(2, 0, 1, 3)).reshape(
        grid_count, 2 * modes_x, rows
    )
    backward = np.ascontiguousarray(turns.transpose(2, 0, 3, 1)).reshape(
        grid_count, 2 * rows, modes_x
    )
    cs = lax.dynamic_index_in_dim(jnp.asarray(forward), grid_index, 0, keepdims=False)
    cs_t = lax.dynamic_index_in_dim(jnp.asarray(backward), grid_index, 0, keepdims=False)
    weight_c = np.where(np.arange(wide) % modes_y == 0, 1.0, 2.0).astype(np.float32)
    weight = jnp.asarray((weight_c / side)[None, :])

    first_local = lax.dynamic_slice_in_dim(core_first, chan_index * chan, chan, 0)
    second_local = lax.dynamic_slice_in_dim(core_second, chan_index * chan, chan, 1)
    first_bf = first_local.astype(BF16)
    second_bf = second_local.astype(BF16)
    pairs = rank_a * rank_b
    second_ab = second_bf.transpose(0, 2, 1).reshape(pairs, chan)
    second_ba = second_bf.transpose(2, 0, 1).reshape(pairs, chan)
    second_t = second_bf.transpose(1, 0, 2).reshape(chan, pairs)
    third_rows = core_third.transpose(1, 0, 2).reshape(modes_x * rank_b, rank_d)
    column = column_mode_core.transpose(1, 0, 2).reshape(rank_d, wide)
    kernel = dot(third_rows, column, HI).reshape(modes_x, rank_b, wide)

    row_steps = rows // STEP
    mode_steps = modes_x // STEP
    chan_step = min(chan, STEP)
    out_step = min(chan, 8)

    row_modes, lead = pl.pallas_call(
        lead_kernel,
        grid=(row_steps,),
        in_specs=[
            whole((rank_a, chan)),
            whole((side, wide)),
            whole((2 * modes_x, rows)),
            pl.BlockSpec((chan, STEP, side), lambda i: (0, i, 0)),
        ],
        out_specs=[
            pl.BlockSpec((chan, STEP, wide), lambda i: (0, i, 0)),
            whole((rank_a, modes_x, wide)),
        ],
        out_shape=[
            jax.ShapeDtypeStruct((chan, rows, wide), BF16),
            jax.ShapeDtypeStruct((rank_a, modes_x, wide), F32),
        ],
        scratch_shapes=[
            pltpu.VMEM((rank_a * STEP, chan * STEP), BF16),
            pltpu.VMEM((rank_a, rows, wide), BF16),
        ],
        compiler_params=params(),
        name="lead",
    )(first_bf.T, table, cs, input_field)

    spec_grad = pl.pallas_call(
        grad_kernel,
        grid=(chan // chan_step,),
        in_specs=[
            whole((side, wide)),
            whole((2 * modes_x, rows)),
            whole((1, wide)),
            pl.BlockSpec((chan_step, rows, side), lambda i: (i, 0, 0)),
        ],
        out_specs=pl.BlockSpec((modes_x, chan_step, wide), lambda i: (0, i, 0)),
        out_shape=jax.ShapeDtypeStruct((modes_x, chan, wide), BF16),
        scratch_shapes=[pltpu.VMEM((chan_step, modes_x, wide), F32)],
        compiler_params=params(),
        name="spec_grad",
    )(table, cs, weight, out_cotangent)

    lead_grad = pl.pallas_call(
        back_kernel,
        grid=(mode_steps,),
        in_specs=[
            whole((pairs, chan)),
            pl.BlockSpec((STEP, rank_b, wide), lambda i: (i, 0, 0)),
            pl.BlockSpec((STEP, chan, wide), lambda i: (i, 0, 0)),
        ],
        out_specs=pl.BlockSpec((rank_a, STEP, wide), lambda i: (0, i, 0)),
        out_shape=jax.ShapeDtypeStruct((rank_a, modes_x, wide), F32),
        scratch_shapes=[pltpu.VMEM((STEP, rank_a, wide), F32)],
        compiler_params=params(),
        name="lead_grad",
    )(second_ba, kernel, spec_grad)
    lead, lead_grad = sum_all([lead, lead_grad], 0)

    spec_out, part_second, part_third, part_fourth = pl.pallas_call(
        mix_kernel,
        grid=(mode_steps,),
        in_specs=[
            pl.BlockSpec((rank_a, STEP, wide), lambda i: (0, i, 0)),
            pl.BlockSpec((STEP, rank_b, wide), lambda i: (i, 0, 0)),
            pl.BlockSpec((STEP, chan, wide), lambda i: (i, 0, 0)),
            whole((pairs, chan)),
            whole((chan, pairs)),
            pl.BlockSpec((STEP * rank_b, rank_d), lambda i: (i, 0)),
            whole((rank_d, wide)),
        ],
        out_specs=[
            pl.BlockSpec((chan, STEP, wide), lambda i: (0, i, 0)),
            whole((chan, pairs)),
            pl.BlockSpec((1, rank_d, STEP * rank_b), lambda i: (i, 0, 0)),
            whole((rank_d, wide)),
        ],
        out_shape=[
            jax.ShapeDtypeStruct((chan, modes_x, wide), BF16),
            jax.ShapeDtypeStruct((chan, pairs), F32),
            jax.ShapeDtypeStruct((mode_steps, rank_d, STEP * rank_b), F32),
            jax.ShapeDtypeStruct((rank_d, wide), F32),
        ],
        scratch_shapes=[
            pltpu.VMEM((STEP, rank_a, wide), F32),
            pltpu.VMEM((pairs, wide), BF16),
            pltpu.VMEM((STEP, chan, wide), F32),
            pltpu.VMEM((STEP * rank_b, wide), F32),
        ],
        compiler_params=params(),
        name="mix",
    )(lead, kernel, spec_grad, second_ab, second_t, third_rows, column)

    back_rows, part_first = pl.pallas_call(
        first_kernel,
        grid=(row_steps,),
        in_specs=[
            whole((2 * rows, modes_x)),
            whole((rank_a, modes_x, wide)),
            pl.BlockSpec((chan, STEP, wide), lambda i: (0, i, 0)),
        ],
        out_specs=[whole((rank_a, rows, wide)), whole((rank_a, chan))],
        out_shape=[
            jax.ShapeDtypeStruct((rank_a, rows, wide), BF16),
            jax.ShapeDtypeStruct((rank_a, chan), F32),
        ],
        scratch_shapes=[pltpu.VMEM((chan * STEP, rank_a * STEP), F32)],
        compiler_params=params(),
        name="first",
    )(cs_t, lead_grad, row_modes)

    first_wide = lax.dynamic_update_slice(
        jnp.zeros((rank_a, channels), F32), part_first * (1.0 / side), (0, chan_index * chan)
    )
    second_wide = lax.dynamic_update_slice(
        jnp.zeros((channels, pairs), F32), part_second, (chan_index * chan, 0)
    )
    sizes = [first_wide.size, second_wide.size, part_third.size, part_fourth.size]
    packed = jnp.concatenate(
        [v.reshape(-1, wide) for v in (first_wide, second_wide, part_third, part_fourth)]
    )
    block = 8 * grid_count * lax.axis_size("chan")
    packed = jnp.pad(packed, ((0, -packed.shape[0] % block), (0, 0)))
    packed = sum_all([packed], 1)[0] * (1.0 / modes_x)
    cuts = np.cumsum([0] + [s // wide for s in sizes])
    one, two, three, four = (packed[cuts[n] : cuts[n + 1]] for n in range(4))
    grad_first = one.reshape(rank_a, channels).T
    grad_second = two.reshape(channels, rank_a, rank_b).transpose(1, 0, 2)
    grad_third = (
        three.reshape(mode_steps, rank_d, STEP, rank_b)
        .transpose(3, 0, 2, 1)
        .reshape(rank_b, modes_x, rank_d)
    )
    grad_fourth = four.reshape(rank_d, 2, modes_y).transpose(1, 0, 2)

    output_field = pl.pallas_call(
        field_kernel,
        grid=(chan // out_step,),
        in_specs=[
            whole((2 * rows, modes_x)),
            whole((wide, side)),
            pl.BlockSpec((out_step, modes_x, wide), lambda i: (i, 0, 0)),
        ],
        out_specs=pl.BlockSpec((out_step, rows, side), lambda i: (i, 0, 0)),
        out_shape=jax.ShapeDtypeStruct((chan, rows, side), BF16),
        scratch_shapes=[pltpu.VMEM((out_step * rows, wide), BF16)],
        compiler_params=params(),
        name="output",
    )(cs_t, table_t, spec_out)

    input_grad = pl.pallas_call(
        input_kernel,
        grid=(row_steps,),
        in_specs=[
            whole((chan, rank_a)),
            whole((wide, side)),
            pl.BlockSpec((rank_a, STEP, wide), lambda i: (0, i, 0)),
        ],
        out_specs=pl.BlockSpec((chan, STEP, side), lambda i: (0, i, 0)),
        out_shape=jax.ShapeDtypeStruct((chan, rows, side), BF16),
        scratch_shapes=[pltpu.VMEM((chan * STEP, rank_a * STEP), BF16)],
        compiler_params=params(),
        name="input_grad",
    )(first_bf, table_t, back_rows)

    return output_field, input_grad, grad_first, grad_second, grad_third, grad_fourth


def solution(mesh):
    placed = (P("chan", "grid", None), P("chan", "grid", None), P(), P(), P(), P())
    return jax.shard_map(
        local,
        mesh=mesh,
        in_specs=placed,
        out_specs=(P("chan", "grid", None), P("chan", "grid", None), P(), P(), P(), P()),
        check_vma=False,
    )
```
